32 devices in a mesh: sub: 16 (over z, y, core), rng: 2 (over x).
Axes of the slice: x: 2, y: 2, z: 4, core: 2. Of those that a mesh axis runs over, the one named last changes fastest.
Arguments:
- image: bfloat16 [2, 4096, 1024], P(None, 'sub', 'rng'), may hold values from -30 to 30
- stencil: int32 [4, 2, 2, 256, 4], replicated, may hold values from 0 to 255, as said below
- interp_weights: float32 [4, 4], replicated, may hold values from 0.25 to 0.6
- range_taps: float32 [4, 2, 3], replicated, may hold values from 0.25 to 0.7
Outputs:
- merged: bfloat16 [2, 4096, 1024], P(None, 'sub', 'rng')
- beam_phase: float32 [2, 4096], P(None, 'sub')
The draws below stay inside these ranges and needn't reach their ends.
Inputs may be any that keep to these rules, and one draw needn't show every extreme that they name: `stencil`: for every section, half, child and beam the 4 indices are consecutive and rising.
All inputs are finite; a program needn't handle non-finite values.
Results may differ from the reference program's by a relative error of at most 0.012.
Values may be sent and summed in bfloat16 or wider, within the bound.
No kernel may reach another device: no remote copies, remote signals or barrier semaphores. Data moves between devices by JAX's collectives and lax.ppermute only.
A program may use at most 64 MiB of HBM per device.

```python
import math
import jax
import jax.numpy as jnp
from jax import lax

ANG = 256
SECTIONS = 4
TAPS = 4
BEAMS = 4096
NR = 1024
N_SUB = 16


def draw_image(key, part):
    first_key = jax.random.fold_in(jax.random.fold_in(key, 11), 0)
    position = jnp.arange(NR, dtype=jnp.float32) / NR
    envelope = jnp.exp(position * math.log(3.0))
    values = jnp.clip(jax.random.normal(first_key, (2, BEAMS, NR), jnp.float32), -3.0, 3.0) * envelope
    return values.astype(jnp.bfloat16)


def draw_stencil(key, part):
    jitter = jax.random.randint(jax.random.fold_in(key, 5), (SECTIONS, 2, 2, ANG, 1), -2, 3)
    centre = (jnp.arange(2, dtype=jnp.int32)[:, None] * ANG + jnp.arange(ANG, dtype=jnp.int32)[None, :]) // 2
    start = jnp.clip(centre.reshape(1, 2, 1, ANG, 1) + jitter - 1, 0, ANG - TAPS)
    return (start + jnp.arange(TAPS, dtype=jnp.int32)).astype(jnp.int32)


def setup_inputs(seed: int = 0) -> dict:
    seeds = jax.random.split(jax.random.key(seed), 5)
    image = draw_image(jax.random.fold_in(seeds[4], 71), 0)
    stencil = draw_stencil(jax.random.fold_in(seeds[4], 71), 0)
    interp_weights = jnp.clip(jax.random.uniform(seeds[2], (SECTIONS, TAPS), jnp.float32, 0.25, 0.6), 0.25, 0.6)
    range_taps = jnp.clip(jax.random.uniform(seeds[3], (SECTIONS, 2, 3), jnp.float32, 0.25, 0.7), 0.25, 0.7)
    return dict(image=image, stencil=stencil, interp_weights=interp_weights, range_taps=range_taps)


epsilon = 1e-06

def coefficients(weights, section_num, beams_dev):
    beam_pos = jnp.arange(beams_dev, dtype=jnp.float32)
    half_pos = jnp.arange(2, dtype=jnp.float32).reshape(2, 1, 1)
    child_sign = (2.0 * jnp.arange(2, dtype=jnp.float32) - 1.0).reshape(1, 2, 1)
    angles = child_sign * (half_pos * beams_dev + beam_pos + 0.5) * (0.37 + 0.11 * section_num)
    weights = weights.astype(jnp.float32)
    real_part = (jnp.cos(angles)[..., None] * weights).astype(jnp.bfloat16)
    imag_part = (jnp.sin(angles)[..., None] * weights).astype(jnp.bfloat16)
    return (real_part, imag_part)

def rotate_rows(blocks, factors):
    values = blocks.astype(jnp.float32)
    real_factor = factors[0][..., None]
    imag_factor = factors[1][..., None]
    real_out = values[0] * real_factor - values[1] * imag_factor
    imag_out = values[0] * imag_factor + values[1] * real_factor
    return jnp.stack([real_out, imag_out]).astype(jnp.bfloat16)

def phase_factors(merged):
    values = merged.astype(jnp.float32)
    following = jnp.roll(values, -1, axis=2)
    lag_real = lax.optimization_barrier(jnp.sum(values[0] * following[0] + values[1] * following[1], axis=-1))
    lag_imag = lax.optimization_barrier(jnp.sum(values[0] * following[1] - values[1] * following[0], axis=-1))
    power = lax.optimization_barrier(jnp.sum((values[0] ** 2 + values[1] ** 2) * (following[0] ** 2 + following[1] ** 2), axis=-1))
    scale = 1.0 / jnp.sqrt(power + epsilon)
    return jnp.stack([lag_real * scale, -lag_imag * scale])

def reference(image, stencil, interp_weights, range_taps):
    blocks = image.reshape(2, N_SUB, ANG, NR)
    merged = blocks
    factors = None
    for section_num in range(SECTIONS):
        if section_num > 0:
            blocks = rotate_rows(merged, factors)
        real_part, imag_part = coefficients(interp_weights[section_num], section_num, ANG)
        span = 2 ** section_num
        source = blocks.astype(jnp.float32)

        def merge_block(block_num):
            half_bit = block_num // span % 2
            first = block_num - half_bit * span
            summed = jnp.zeros((2, ANG, NR), jnp.float32)
            for child_num in range(2):
                child = lax.dynamic_index_in_dim(source, first + child_num * span, 1, keepdims=False)
                indices = lax.dynamic_index_in_dim(stencil[section_num, :, child_num], half_bit, 0, keepdims=False)
                coef_re = lax.dynamic_index_in_dim(real_part[:, child_num], half_bit, 0, keepdims=False).astype(jnp.float32)
                coef_im = lax.dynamic_index_in_dim(imag_part[:, child_num], half_bit, 0, keepdims=False).astype(jnp.float32)
                picked = child[:, indices]
                part_re = lax.optimization_barrier(jnp.sum(coef_re[..., None] * picked[0] - coef_im[..., None] * picked[1], axis=1))
                part_im = lax.optimization_barrier(jnp.sum(coef_re[..., None] * picked[1] + coef_im[..., None] * picked[0], axis=1))
                padded = jnp.pad(jnp.stack([part_re, part_im]), ((0, 0), (0, 0), (1, 1)))
                for tap_num in range(3):
                    summed = summed + range_taps[section_num, child_num, tap_num] * padded[:, :, tap_num:tap_num + NR]
            return summed.astype(jnp.bfloat16)
        merged = lax.map(merge_block, jnp.arange(N_SUB, dtype=jnp.int32))
        merged = jnp.transpose(merged, (1, 0, 2, 3))
        factors = phase_factors(merged)
    return (merged.reshape(2, BEAMS, NR), factors.reshape(2, BEAMS))
```

```python
import functools

import jax
import jax.numpy as jnp
from jax import lax
from jax.experimental import pallas as pl
from jax.experimental.pallas import tpu as pltpu
from jax.sharding import PartitionSpec as P

SECTIONS = 4
TAPS = 4
LANES = 128
epsilon = 1e-06

FORWARD = (True, True, False, False)
SKEW_IN = (0, 1, 2, 1)
CHUNKS = 4
CALLS = (((0, 1, 2, 3),), ((0,), (1,), (2,), (3,)), ((3, 2, 1, 0),), ((3,), (2,), (1,), (0,)))

f32 = jnp.float32
bf16 = jnp.bfloat16
NT = (((1,), (1,)), ((), ()))
VMEM = pl.BlockSpec(memory_space=pltpu.VMEM)


def params(mib=16):
    return pltpu.CompilerParams(vmem_limit_bytes=mib << 20)


def call(kernel, out_shape, name, args, out_specs=None, in_specs=None, scratch=(), aliases=None, flops=0):
    outs = jax.tree.leaves(out_shape)
    nbytes = sum(a.size * a.dtype.itemsize for a in list(args) + outs)
    return pl.pallas_call(
        kernel,
        out_shape=out_shape,
        in_specs=in_specs or [VMEM] * len(args),
        out_specs=out_specs or jax.tree.map(lambda _: VMEM, out_shape),
        scratch_shapes=list(scratch),
        input_output_aliases=aliases or {},
        compiler_params=params(),
        cost_estimate=pl.CostEstimate(flops=flops, bytes_accessed=nbytes, transcendentals=0),
        name=name,
    )(*args)


def shape(dims, dtype):
    return jax.ShapeDtypeStruct(dims, dtype)


def pair_matrix(out_ref, child, real, imag):
    beams = real.shape[0]
    out_ref[child, :beams, :beams] = real.astype(bf16)
    out_ref[child, :beams, beams:] = (-imag).astype(bf16)
    out_ref[child, beams:, :beams] = imag.astype(bf16)
    out_ref[child, beams:, beams:] = real.astype(bf16)


def build_kernel(sections, full, stencil_ref, weights_ref, out_ref, rows_ref):
    sub = lax.axis_index("sub")
    beams = stencil_ref.shape[-1]
    beam = lax.broadcasted_iota(jnp.int32, (1, beams), 1).astype(f32)
    rows_ref[...] = jnp.zeros_like(rows_ref)
    for k, s in enumerate(sections):
        half = (sub >> s) & 1
        angle = (half.astype(f32) * beams + beam + 0.5) * (0.37 + 0.11 * s)
        sign = 2.0 * half.astype(f32) - 1.0
        cosine = jnp.cos(angle)
        sine = jnp.sin(angle) * sign
        for t in range(TAPS):
            weight = weights_ref[s : s + 1, t : t + 1]
            rows_ref[16 * k + t : 16 * k + t + 1, :] = cosine * weight
            rows_ref[16 * k + 4 + t : 16 * k + 5 + t, :] = sine * weight
        rows_ref[16 * k + 8 : 16 * k + 9, :] = stencil_ref[s, half, half, 0:1, :].astype(f32)
        rows_ref[16 * k + 9 : 16 * k + 10, :] = stencil_ref[s, half, 1 - half, 0:1, :].astype(f32)
    row = lax.broadcasted_iota(jnp.int32, (beams, beams), 0)
    column = lax.broadcasted_iota(jnp.int32, (beams, beams), 1)
    identity = jnp.where(row == column, 1.0, 0.0).astype(bf16)
    columns = lax.dot_general(
        identity, rows_ref[...].astype(bf16), NT, preferred_element_type=f32
    )
    place = column.astype(f32)
    for k, s in enumerate(sections):
        table = columns[:, 16 * k : 16 * k + 16]
        for child in range(2):
            step = place - table[:, 8 + child : 9 + child]
            real = jnp.zeros((beams, beams), f32)
            imag = jnp.zeros((beams, beams), f32)
            for t in range(TAPS):
                hit = step == float(t)
                real = jnp.where(hit, table[:, t : t + 1], real)
                imag = jnp.where(hit, table[:, 4 + t : 5 + t], imag)
            if child == 1:
                imag = -imag
            if full:
                pair_matrix(out_ref, child, real, imag)
            else:
                out_ref[k, child, 0] = real.astype(bf16)
                out_ref[k, child, 1] = imag.astype(bf16)


def build(sections, full, stencil, weights):
    beams = stencil.shape[-1]
    if full:
        out = shape((2, 2 * beams, 2 * beams), bf16)
    else:
        out = shape((len(sections), 2, 2, beams, beams), bf16)
    return call(
        functools.partial(build_kernel, sections, full),
        out,
        "build",
        (stencil, weights),
        scratch=[pltpu.VMEM((16 * len(sections), beams), f32)],
    )


def edge_rows(forward, tile):
    both = jnp.concatenate([tile[0], tile[1]], axis=1)
    row = lax.broadcasted_iota(jnp.int32, (8, 2 * LANES), 0)
    lane = lax.broadcasted_iota(jnp.int32, (8, 2 * LANES), 1)
    first = LANES - 2 if forward else 0
    wanted = (row - 4) // 2 * LANES + first + (row - 4) % 2
    pick = jnp.where((row >= 4) & (lane == wanted), 1.0, 0.0).astype(bf16)
    return lax.dot_general(pick, both, NT, preferred_element_type=f32)


def edge_kernel(forward, image_ref, out_ref):
    columns = image_ref.shape[-1]
    begin = columns - LANES if forward else 0
    out_ref[...] = edge_rows(forward, image_ref[:, :, begin : begin + LANES])


def tap_values(s, taps_ref):
    half = (lax.axis_index("sub") >> s) & 1
    own, other = [], []
    for k in range(3):
        zero = taps_ref[k, 0:1, s : s + 1]
        one = taps_ref[k, 1:2, s : s + 1]
        own.append(jnp.where(half == 1, one, zero))
        other.append(jnp.where(half == 1, zero, one))
    return own, other


def carry_of(s, matrix_ref, taps_ref, edges):
    forward = FORWARD[s]
    beams = matrix_ref.shape[1] // 2
    own, other = tap_values(s, taps_ref)
    products = []
    for child in range(2):
        rows = jnp.concatenate(
            [
                jnp.concatenate([edges[child][4:5], edges[child][6:7]], axis=1),
                jnp.concatenate([edges[child][5:6], edges[child][7:8]], axis=1),
                jnp.zeros((LANES - 2, 2 * beams), f32),
            ],
            axis=0,
        ).astype(bf16)
        products.append(
            lax.dot_general(matrix_ref[child], rows, NT, preferred_element_type=f32)
        )
    lower, middle, upper = [own[k] * products[0] + other[k] * products[1] for k in range(3)]
    lane = lax.broadcasted_iota(jnp.int32, lower.shape, 1)
    rng = lax.axis_index("rng")
    last = lax.axis_size("rng") - 1
    if forward:
        inner = jnp.where((rng == 0) & (s == 0), 0.0, 1.0)
        near = pltpu.roll(middle, LANES - 1, 1) + lower
        far = pltpu.roll(lower, 0, 1) * inner
        return jnp.where(lane == 0, near, jnp.where(lane == 1, far, 0.0))
    inner = jnp.where((rng == last) & (s == 3), 0.0, 1.0)
    near = pltpu.roll(middle, LANES - 1, 1) + pltpu.roll(upper, LANES - 2, 1) * inner
    far = pltpu.roll(upper, LANES - 2, 1)
    return jnp.where(lane == LANES - 1, near, jnp.where(lane == LANES - 2, far, 0.0))


def start_kernel(matrix_ref, taps_ref, own_ref, other_ref, carry_ref):
    carry_ref[...] = carry_of(0, matrix_ref, taps_ref, (own_ref[...], other_ref[...]))


def prep_kernel(s, ranks, parts_ref, taps_ref, *refs):
    own_refs, other_refs = refs[:ranks], refs[ranks : 2 * ranks]
    matrix_ref, carry_ref = refs[2 * ranks :]
    beams = parts_ref.shape[-1]
    edges = []
    for child, group in enumerate((own_refs, other_refs)):
        total = group[0][0:4]
        for ref in group[1:]:
            total = total + ref[0:4]
        scale = 1.0 / jnp.sqrt(total[2:3] + epsilon)
        factor_re = total[0:1] * scale
        factor_im = -total[1:2] * scale
        real = parts_ref[child, 0].astype(f32)
        imag = parts_ref[child, 1].astype(f32)
        pair_matrix(
            matrix_ref,
            child,
            real * factor_re - imag * factor_im,
            real * factor_im + imag * factor_re,
        )
        edges.append(group[ranks - 1 if FORWARD[s] else 1 % ranks][...])
    carry_ref[...] = carry_of(s, matrix_ref, taps_ref, edges)


def section_kernel(s, chunks, width, total, whole, aliased, refs):
    n = len(chunks)
    matrix_ref, taps_ref, carry_ref, stats_ref = refs[:4]
    given = 1 if whole else n
    if whole:
        own_refs = [refs[4].at[:, :, c * width : (c + 1) * width] for c in chunks]
        other_refs = [refs[5].at[:, :, c * width : (c + 1) * width] for c in chunks]
    else:
        own_refs, other_refs = refs[4 : 4 + n], refs[4 + n : 4 + 2 * n]
    rest = refs[4 + 2 * given + aliased :]
    if s + 1 == SECTIONS:
        target_ref, carry_out, stats_out, buffer_ref, sem = rest
        out_refs = [buffer_ref.at[i] for i in range(n)]
    else:
        out_refs, carry_out, stats_out = rest[:n], rest[n], rest[n + 1]
    copies = []
    forward, skew = FORWARD[s], SKEW_IN[s]
    own, other = tap_values(s, taps_ref)
    beams = matrix_ref.shape[1] // 2
    first_rank = lax.axis_index("rng") == 0
    lane = lax.broadcasted_iota(jnp.int32, (1, width), 1)
    carry = carry_ref[...]
    stats = stats_ref[...]
    row8 = lax.broadcasted_iota(jnp.int32, (8, 3 * LANES), 0)
    lane8 = lax.broadcasted_iota(jnp.int32, (8, 3 * LANES), 1)
    summing = jnp.where(lane8 // LANES == row8, 1.0, 0.0)
    for i, chunk in enumerate(chunks):
        own_terms = jnp.dot(
            matrix_ref[0], own_refs[i][...].reshape(2 * beams, width), preferred_element_type=f32
        )
        other_terms = jnp.dot(
            matrix_ref[1], other_refs[i][...].reshape(2 * beams, width), preferred_element_type=f32
        )
        lower, middle, upper = [own[k] * own_terms + other[k] * other_terms for k in range(3)]
        edge = chunk == 0

        def without(array, place):
            if not edge:
                return array
            return jnp.where(first_rank & (lane == place), 0.0, array)

        if forward:
            upper = without(upper, skew)
            rolled1 = pltpu.roll(middle, 1, 1)
            rolled2 = pltpu.roll(lower, 2, 1)
            kept2 = rolled2 if skew == 0 else without(rolled2, skew + 1)
            value = upper + jnp.where(lane >= 1, rolled1, 0.0) + jnp.where(lane >= 2, kept2, 0.0)
            piece = slice(0, LANES)
            lane1 = lane[:, piece]
            following = jnp.where(lane1 < 1, rolled1[:, piece], 0.0) + jnp.where(
                lane1 < 2, rolled2[:, piece], 0.0
            )
        else:
            lower = without(lower, skew - 1)
            rolled1 = pltpu.roll(middle, width - 1, 1)
            rolled2 = pltpu.roll(upper, width - 2, 1)
            kept2 = without(rolled2, skew - 2) if skew >= 2 else rolled2
            value = (
                lower
                + jnp.where(lane < width - 1, rolled1, 0.0)
                + jnp.where(lane < width - 2, kept2, 0.0)
            )
            piece = slice(width - LANES, width)
            lane1 = lane[:, piece]
            following = jnp.where(lane1 >= width - 1, rolled1[:, piece], 0.0) + jnp.where(
                lane1 >= width - 2, rolled2[:, piece], 0.0
            )
        if width == LANES:
            value = value + carry
        elif forward:
            value = jnp.concatenate([value[:, :LANES] + carry, value[:, LANES:]], axis=1)
        else:
            value = jnp.concatenate([value[:, : width - LANES], value[:, width - LANES :] + carry], axis=1)
        carry = following
        merged = value.astype(bf16)
        out_refs[i][0] = merged[:beams]
        out_refs[i][1] = merged[beams:]
        if s + 1 == SECTIONS:
            place = target_ref.at[:, :, chunk * width : (chunk + 1) * width]
            copies.append(pltpu.make_async_copy(buffer_ref.at[i], place, sem.at[i]))
            copies[-1].start()
        v0 = merged[:beams].astype(f32)
        v1 = merged[beams:].astype(f32)
        f0 = pltpu.roll(v0, beams - 1, 0)
        f1 = pltpu.roll(v1, beams - 1, 0)
        lag_real = v0 * f0 + v1 * f1
        lag_imag = v0 * f1 - v1 * f0
        power = (v0 * v0 + v1 * v1) * (f0 * f0 + f1 * f1)
        folded = []
        for sums in (lag_real, lag_imag, power):
            part = sums[:, :LANES]
            for k in range(1, width // LANES):
                part = part + sums[:, k * LANES : (k + 1) * LANES]
            folded.append(part)
        stats = stats + lax.dot_general(
            summing,
            jnp.concatenate(folded, axis=1),
            NT,
            precision=lax.Precision.HIGHEST,
            preferred_element_type=f32,
        )
        if s + 1 < SECTIONS:
            onward = FORWARD[s + 1]
            if chunk == (total - 1 if onward else 0):
                begin = width - LANES if onward else 0
                stats = stats + edge_rows(
                    onward,
                    (merged[:beams, begin : begin + LANES], merged[beams:, begin : begin + LANES]),
                )
    carry_out[...] = carry
    stats_out[...] = stats
    for copy in copies:
        copy.wait()


def section(s, chunks, total, width, matrix, taps, carry, stats, own, other, target=None):
    n = len(chunks)
    beams = matrix.shape[1] // 2
    args = [matrix, taps, carry, stats]
    specs = [VMEM] * 4
    whole = not isinstance(own, list)
    for group in (own, other):
        for array in [group] if whole else [group[chunk] for chunk in chunks]:
            args.append(array)
            specs.append(VMEM)
    aliases = {}
    scratch = []
    if s + 1 == SECTIONS:
        outs = [shape((2, beams, total * width), bf16)]
        blocks = [pl.BlockSpec(memory_space=pl.ANY)]
        scratch = [pltpu.VMEM((n, 2, beams, width), bf16), pltpu.SemaphoreType.DMA((n,))]
        if target is not None:
            aliases = {len(args): 0}
            args.append(target)
            specs.append(pl.BlockSpec(memory_space=pl.ANY))
    else:
        outs = [shape((2, beams, width), bf16)] * n
        blocks = [VMEM] * n
    outs = outs + [shape((2 * beams, LANES), f32), shape((8, beams), f32)]
    blocks = blocks + [VMEM] * 2
    result = call(
        lambda *refs: section_kernel(s, chunks, width, total, whole, len(aliases), refs),
        outs,
        f"section{s}",
        args,
        out_specs=blocks,
        in_specs=specs,
        scratch=scratch,
        aliases=aliases,
        flops=n * 2 * 2 * (2 * beams) ** 2 * width,
    )
    return result[: len(result) - 2], result[-2], result[-1]


def factor_kernel(ranks, *refs):
    out_ref = refs[ranks]
    total = refs[0][...]
    for ref in refs[1:ranks]:
        total = total + ref[...]
    scale = 1.0 / jnp.sqrt(total[2:3] + epsilon)
    out_ref[0:1, :] = total[0:1] * scale
    out_ref[1:2, :] = -total[1:2] * scale


def swap(value, s, shift=0):
    size, ranks = lax.axis_size("sub"), lax.axis_size("rng")
    mask = 0 if s is None else 2**s
    pairs = []
    for b in range(size):
        for r in range(ranks):
            pairs.append(((b ^ mask) * ranks + (r + shift) % ranks, b * ranks + r))
    return lax.ppermute(value, ("sub", "rng"), pairs)


def on_device(image, stencil, interp_weights, range_taps):
    beams, columns = image.shape[1:]
    ranks = lax.axis_size("rng")
    total = CHUNKS
    width = columns // total
    table = jnp.transpose(stencil, (0, 1, 2, 4, 3))
    taps = jnp.transpose(range_taps, (2, 1, 0))
    rows = call(functools.partial(edge_kernel, FORWARD[0]), shape((8, beams), f32), "edge", (image,))
    back = ranks - 1
    edge_own = swap(rows, None, back)
    edge_other = swap(rows, 0, back)
    partner = swap(image, 0)
    matrix = build((0,), True, table, interp_weights)
    parts = build((1, 2, 3), False, table, interp_weights)
    carry = call(
        start_kernel, shape((2 * beams, LANES), f32), "start", (matrix, taps, edge_own, edge_other)
    )
    own, other = image, partner
    for s in range(SECTIONS):
        stats = jnp.zeros((8, beams), f32)
        merged, received = [None] * total, [None] * total
        target = None
        for chunks in CALLS[s]:
            outs, carry, stats = section(
                s, chunks, total, width, matrix, taps, carry, stats, own, other, target
            )
            if s + 1 == SECTIONS:
                target = outs[0]
                continue
            for chunk, array in zip(chunks, outs):
                merged[chunk] = array
                received[chunk] = swap(array, s + 1)
        others = [swap(stats, None, d) for d in range(1, ranks)]
        if s + 1 == SECTIONS:
            factors = call(
                functools.partial(factor_kernel, ranks), shape((2, beams), f32), "factor", [stats] + others
            )
            return target, factors
        partners = [swap(stats, s + 1, d) for d in range(ranks)]
        matrix, carry = call(
            functools.partial(prep_kernel, s + 1, ranks),
            [shape((2, 2 * beams, 2 * beams), bf16), shape((2 * beams, LANES), f32)],
            "prep",
            [parts[s], taps, stats, *others, *partners],
        )
        own, other = merged, received


def solution(mesh):
    placed = (P(None, "sub", "rng"), P(), P(), P())
    return jax.shard_map(
        on_device,
        mesh=mesh,
        in_specs=placed,
        out_specs=(P(None, "sub", "rng"), P(None, "sub")),
        check_vma=False,
    )
```

```python
import functools

import jax
import jax.numpy as jnp
from jax import lax
from jax.experimental import pallas as pl
from jax.experimental.pallas import tpu as pltpu
from jax.sharding import PartitionSpec as P

SECTIONS = 4
TAPS = 4
LANES = 128
epsilon = 1e-06

FORWARD = (True, True, False, False)
SKEW_IN = (0, 1, 2, 1)
CHUNKS = 4
CALLS = (((1,), (2,), (3, 0)), ((1,), (2,), (3,), (0,)), ((3,), (2,), (1,), (0,)), ((3,), (2,), (1,), (0,)))


f32 = jnp.float32
bf16 = jnp.bfloat16
NT = (((1,), (1,)), ((), ()))
VMEM = pl.BlockSpec(memory_space=pltpu.VMEM)


def params(mib=16):
    return pltpu.CompilerParams(vmem_limit_bytes=mib << 20)


def call(kernel, out_shape, args, out_specs=None, in_specs=None, scratch=(), aliases=None, flops=0):
    outs = jax.tree.leaves(out_shape)
    nbytes = sum(a.size * a.dtype.itemsize for a in list(args) + outs)
    return pl.pallas_call(
        kernel,
        out_shape=out_shape,
        in_specs=in_specs or [VMEM] * len(args),
        out_specs=out_specs or jax.tree.map(lambda _: VMEM, out_shape),
        scratch_shapes=list(scratch),
        input_output_aliases=aliases or {},
        compiler_params=params(),
        cost_estimate=pl.CostEstimate(flops=flops, bytes_accessed=nbytes, transcendentals=0),
    )(*args)


def shape(dims, dtype):
    return jax.ShapeDtypeStruct(dims, dtype)


def pair_matrix(out_ref, child, real, imag):
    beams = real.shape[0]
    out_ref[child, :beams, :beams] = real.astype(bf16)
    out_ref[child, :beams, beams:] = (-imag).astype(bf16)
    out_ref[child, beams:, :beams] = imag.astype(bf16)
    out_ref[child, beams:, beams:] = real.astype(bf16)


def build_kernel(sections, full, stencil_ref, weights_ref, out_ref, rows_ref):
    sub = lax.axis_index("sub")
    beams = stencil_ref.shape[-1]
    beam = lax.broadcasted_iota(jnp.int32, (1, beams), 1).astype(f32)
    rows_ref[...] = jnp.zeros_like(rows_ref)
    for k, s in enumerate(sections):
        half = (sub >> s) & 1
        angle = (half.astype(f32) * beams + beam + 0.5) * (0.37 + 0.11 * s)
        sign = 2.0 * half.astype(f32) - 1.0
        cosine = jnp.cos(angle)
        sine = jnp.sin(angle) * sign
        for t in range(TAPS):
            weight = weights_ref[s : s + 1, t : t + 1]
            rows_ref[16 * k + t : 16 * k + t + 1, :] = cosine * weight
            rows_ref[16 * k + 4 + t : 16 * k + 5 + t, :] = sine * weight
        rows_ref[16 * k + 8 : 16 * k + 9, :] = stencil_ref[s, half, half, 0:1, :].astype(f32)
        rows_ref[16 * k + 9 : 16 * k + 10, :] = stencil_ref[s, half, 1 - half, 0:1, :].astype(f32)
    row = lax.broadcasted_iota(jnp.int32, (beams, beams), 0)
    column = lax.broadcasted_iota(jnp.int32, (beams, beams), 1)
    identity = jnp.where(row == column, 1.0, 0.0).astype(bf16)
    columns = lax.dot_general(
        identity, rows_ref[...].astype(bf16), NT, preferred_element_type=f32
    )
    place = column.astype(f32)
    for k, s in enumerate(sections):
        table = columns[:, 16 * k : 16 * k + 16]
        for child in range(2):
            step = place - table[:, 8 + child : 9 + child]
            real = jnp.zeros((beams, beams), f32)
            imag = jnp.zeros((beams, beams), f32)
            for t in range(TAPS):
                hit = step == float(t)
                real = jnp.where(hit, table[:, t : t + 1], real)
                imag = jnp.where(hit, table[:, 4 + t : 5 + t], imag)
            if child == 1:
                imag = -imag
            if full:
                pair_matrix(out_ref, child, real, imag)
            else:
                out_ref[k, child, 0] = real.astype(bf16)
                out_ref[k, child, 1] = imag.astype(bf16)


def build(sections, full, stencil, weights):
    beams = stencil.shape[-1]
    if full:
        out = shape((2, 2 * beams, 2 * beams), bf16)
    else:
        out = shape((len(sections), 2, 2, beams, beams), bf16)
    return call(
        functools.partial(build_kernel, sections, full),
        out,
        (stencil, weights),
        scratch=[pltpu.VMEM((16 * len(sections), beams), f32)],
    )


def edge_rows(forward, tile):
    both = jnp.concatenate([tile[0], tile[1]], axis=1)
    row = lax.broadcasted_iota(jnp.int32, (8, 2 * LANES), 0)
    lane = lax.broadcasted_iota(jnp.int32, (8, 2 * LANES), 1)
    first = LANES - 2 if forward else 0
    wanted = (row - 4) // 2 * LANES + first + (row - 4) % 2
    pick = jnp.where((row >= 4) & (lane == wanted), 1.0, 0.0).astype(bf16)
    return lax.dot_general(pick, both, NT, preferred_element_type=f32)


def edge_kernel(forward, image_ref, out_ref):
    columns = image_ref.shape[-1]
    begin = columns - LANES if forward else 0
    out_ref[...] = edge_rows(forward, image_ref[:, :, begin : begin + LANES])


def tap_values(s, taps_ref):
    half = (lax.axis_index("sub") >> s) & 1
    own, other = [], []
    for k in range(3):
        zero = taps_ref[k, 0:1, s : s + 1]
        one = taps_ref[k, 1:2, s : s + 1]
        own.append(jnp.where(half == 1, one, zero))
        other.append(jnp.where(half == 1, zero, one))
    return own, other


def carry_of(s, matrix_ref, taps_ref, edges, outer=True):
    forward = FORWARD[s]
    beams = matrix_ref.shape[1] // 2
    own, other = tap_values(s, taps_ref)
    products = []
    for child in range(2):
        rows = jnp.concatenate(
            [
                jnp.concatenate([edges[child][4:5], edges[child][6:7]], axis=1),
                jnp.concatenate([edges[child][5:6], edges[child][7:8]], axis=1),
                jnp.zeros((LANES - 2, 2 * beams), f32),
            ],
            axis=0,
        ).astype(bf16)
        products.append(
            lax.dot_general(matrix_ref[child], rows, NT, preferred_element_type=f32)
        )
    lower, middle, upper = [own[k] * products[0] + other[k] * products[1] for k in range(3)]
    lane = lax.broadcasted_iota(jnp.int32, lower.shape, 1)
    rng = lax.axis_index("rng")
    last = lax.axis_size("rng") - 1
    if forward:
        inner = jnp.where((rng == 0) & (s == 0), 0.0, 1.0) if outer else 1.0
        near = pltpu.roll(middle, LANES - 1, 1) + lower
        far = lower * inner
        return jnp.where(lane == 0, near, jnp.where(lane == 1, far, 0.0))
    inner = jnp.where((rng == last) & (s == 3), 0.0, 1.0)
    near = pltpu.roll(middle, LANES - 1, 1) + pltpu.roll(upper, LANES - 2, 1) * inner
    far = pltpu.roll(upper, LANES - 2, 1)
    return jnp.where(lane == LANES - 1, near, jnp.where(lane == LANES - 2, far, 0.0))


def start_kernel(matrix_ref, taps_ref, own_ref, other_ref, carry_ref):
    carry_ref[...] = carry_of(0, matrix_ref, taps_ref, (own_ref[...], other_ref[...]))


def prep_kernel(s, ranks, parts_ref, taps_ref, *refs):
    own_refs, other_refs = refs[:ranks], refs[ranks : 2 * ranks]
    matrix_ref, carry_ref = refs[2 * ranks : 2 * ranks + 2]
    edges = []
    for child, group in enumerate((own_refs, other_refs)):
        total = group[0][0:4]
        for ref in group[1:]:
            total = total + ref[0:4]
        scale = 1.0 / jnp.sqrt(total[2:3] + epsilon)
        factor_re = total[0:1] * scale
        factor_im = -total[1:2] * scale
        real = parts_ref[child, 0].astype(f32)
        imag = parts_ref[child, 1].astype(f32)
        pair_matrix(
            matrix_ref,
            child,
            real * factor_re - imag * factor_im,
            real * factor_im + imag * factor_re,
        )
        edges.append(group[ranks - 1 if FORWARD[s] else 1 % ranks][0:8])
    carry_ref[...] = carry_of(s, matrix_ref, taps_ref, edges)
    if FORWARD[s]:
        inner_ref = refs[2 * ranks + 2]
        edges = (own_refs[0][8:16], other_refs[0][8:16])
        inner_ref[...] = carry_of(s, matrix_ref, taps_ref, edges, False)


def sum_rows(sums):
    lane = lax.broadcasted_iota(jnp.int32, sums[0].shape, 1)
    table = jnp.zeros(sums[0].shape, f32)
    for k, part in enumerate(sums):
        table = jnp.where(lane == k, jnp.sum(part, axis=1, keepdims=True), table)
    return jnp.transpose(table)[:8]


def section_kernel(s, chunks, width, total, whole, first, last, aliased, refs):
    n = len(chunks)
    matrix_ref, taps_ref = refs[:2]
    refs = list(refs[2:])
    carry_ref = None if first and s == 0 else refs.pop(0)
    outer_ref = refs.pop(0) if FORWARD[s] and 0 in chunks else None
    sums_ref = None if first else refs.pop(0)
    given = 1 if whole else n
    if whole:
        own_refs = [refs[0].at[:, :, c * width : (c + 1) * width] for c in chunks]
        other_refs = [refs[1].at[:, :, c * width : (c + 1) * width] for c in chunks]
    else:
        own_refs, other_refs = refs[:n], refs[n : 2 * n]
    rest = refs[2 * given + aliased :]
    if s + 1 == SECTIONS:
        sem, buffer_ref, target_ref = rest.pop(), rest.pop(), rest.pop(0)
        out_refs = [buffer_ref.at[i] for i in range(n)]
    else:
        out_refs, rest = rest[:n], rest[n:]
    if last:
        (stats_out,) = rest
    else:
        carry_out, sums_out = rest
    copies = []
    forward, skew = FORWARD[s], SKEW_IN[s]
    own, other = tap_values(s, taps_ref)
    beams = matrix_ref.shape[1] // 2
    first_rank = lax.axis_index("rng") == 0
    lane = lax.broadcasted_iota(jnp.int32, (1, width), 1)
    if carry_ref is None:
        edges = [edge_rows(True, ref.at[:, :, width - LANES : width]) for ref in refs[:2]]
        carry = carry_of(s, matrix_ref, taps_ref, edges, False)
    else:
        carry = carry_ref[...]
    sums = [sums_ref[k] for k in range(3)] if sums_ref is not None else None
    edges = {}
    for i, chunk in enumerate(chunks):
        if forward and chunk == 0:
            carry = outer_ref[...]
        own_terms = jnp.dot(
            matrix_ref[0], own_refs[i][...].reshape(2 * beams, width), preferred_element_type=f32
        )
        other_terms = jnp.dot(
            matrix_ref[1], other_refs[i][...].reshape(2 * beams, width), preferred_element_type=f32
        )
        lower, middle, upper = [own[k] * own_terms + other[k] * other_terms for k in range(3)]
        edge = chunk == 0

        def without(array, place):
            if not edge:
                return array
            return jnp.where(first_rank & (lane == place), 0.0, array)

        if forward:
            upper = without(upper, skew)
            rolled1 = pltpu.roll(middle, 1, 1)
            rolled2 = pltpu.roll(lower, 2, 1)
            kept2 = rolled2 if skew == 0 else without(rolled2, skew + 1)
            value = upper + jnp.where(lane >= 1, rolled1, 0.0) + jnp.where(lane >= 2, kept2, 0.0)
            piece = slice(0, LANES)
            lane1 = lane[:, piece]
            following = jnp.where(lane1 < 1, rolled1[:, piece], 0.0) + jnp.where(
                lane1 < 2, rolled2[:, piece], 0.0
            )
        else:
            lower = without(lower, skew - 1)
            rolled1 = pltpu.roll(middle, width - 1, 1)
            rolled2 = pltpu.roll(upper, width - 2, 1)
            kept2 = without(rolled2, skew - 2) if skew >= 2 else rolled2
            value = (
                lower
                + jnp.where(lane < width - 1, rolled1, 0.0)
                + jnp.where(lane < width - 2, kept2, 0.0)
            )
            piece = slice(width - LANES, width)
            lane1 = lane[:, piece]
            following = jnp.where(lane1 >= width - 1, rolled1[:, piece], 0.0) + jnp.where(
                lane1 >= width - 2, rolled2[:, piece], 0.0
            )
        if width == LANES:
            value = value + carry
        elif forward:
            value = jnp.concatenate([value[:, :LANES] + carry, value[:, LANES:]], axis=1)
        else:
            value = jnp.concatenate([value[:, : width - LANES], value[:, width - LANES :] + carry], axis=1)
        carry = following
        merged = value.astype(bf16)
        out_refs[i][0] = merged[:beams]
        out_refs[i][1] = merged[beams:]
        if s + 1 == SECTIONS:
            place = target_ref.at[:, :, chunk * width : (chunk + 1) * width]
            copies.append(pltpu.make_async_copy(buffer_ref.at[i], place, sem.at[i]))
            copies[-1].start()
        v0 = merged[:beams].astype(f32)
        v1 = merged[beams:].astype(f32)
        f0 = pltpu.roll(v0, beams - 1, 0)
        f1 = pltpu.roll(v1, beams - 1, 0)
        lag_real = v0 * f0 + v1 * f1
        lag_imag = v0 * f1 - v1 * f0
        power = (v0 * v0 + v1 * v1) * (f0 * f0 + f1 * f1)
        folded = []
        for product in (lag_real, lag_imag, power):
            part = product[:, :LANES]
            for k in range(1, width // LANES):
                part = part + product[:, k * LANES : (k + 1) * LANES]
            folded.append(part)
        sums = folded if sums is None else [x + y for x, y in zip(sums, folded)]
        edges[chunk] = merged.reshape(2, beams, width)
    if last:
        stats = sum_rows(sums)
        if s + 1 < SECTIONS:
            onward = FORWARD[s + 1]
            begin = width - LANES if onward else 0
            stats = stats + edge_rows(
                onward, edges[total - 1 if onward else 0][:, :, begin : begin + LANES]
            )
            if onward:
                inner = edge_rows(onward, edges[0][:, :, width - LANES :])
                stats = jnp.concatenate([stats, inner], axis=0)
        stats_out[...] = stats
    else:
        carry_out[...] = carry
        for k in range(3):
            sums_out[k] = sums[k]
    for copy in copies:
        copy.wait()


def section(s, chunks, total, width, matrix, taps, carry, outer, sums, own, other, target=None):
    n = len(chunks)
    beams = matrix.shape[1] // 2
    first = sums is None
    last = chunks == CALLS[s][-1]
    args = [matrix, taps]
    if carry is not None:
        args.append(carry)
    if FORWARD[s] and 0 in chunks:
        args.append(outer)
    if not first:
        args.append(sums)
    specs = [VMEM] * len(args)
    whole = not isinstance(own, list)
    for group in (own, other):
        for array in [group] if whole else [group[chunk] for chunk in chunks]:
            args.append(array)
            specs.append(VMEM)
    aliases = {}
    scratch = []
    if s + 1 == SECTIONS:
        outs = [shape((2, beams, total * width), bf16)]
        blocks = [pl.BlockSpec(memory_space=pl.ANY)]
        scratch = [pltpu.VMEM((n, 2, beams, width), bf16), pltpu.SemaphoreType.DMA((n,))]
        if target is not None:
            aliases = {len(args): 0}
            args.append(target)
            specs.append(pl.BlockSpec(memory_space=pl.ANY))
    else:
        outs = [shape((2, beams, width), bf16)] * n
        blocks = [VMEM] * n
    images = len(outs)
    if last:
        rows = 16 if s + 1 < SECTIONS and FORWARD[s + 1] else 8
        outs = outs + [shape((rows, beams), f32)]
    else:
        outs = outs + [shape((2 * beams, LANES), f32), shape((3, beams, LANES), f32)]
    blocks = blocks + [VMEM] * (len(outs) - images)
    result = call(
        lambda *refs: section_kernel(s, chunks, width, total, whole, first, last, len(aliases), refs),
        outs,
        args,
        out_specs=blocks,
        in_specs=specs,
        scratch=scratch,
        aliases=aliases,
        flops=n * 2 * 2 * (2 * beams) ** 2 * width,
    )
    return result[:images], result[images:]


def factor_kernel(ranks, *refs):
    out_ref = refs[ranks]
    total = refs[0][...]
    for ref in refs[1:ranks]:
        total = total + ref[...]
    scale = 1.0 / jnp.sqrt(total[2:3] + epsilon)
    out_ref[0:1, :] = total[0:1] * scale
    out_ref[1:2, :] = -total[1:2] * scale


def swap(value, s, shift=0):
    size, ranks = lax.axis_size("sub"), lax.axis_size("rng")
    mask = 0 if s is None else 2**s
    pairs = []
    for b in range(size):
        for r in range(ranks):
            pairs.append(((b ^ mask) * ranks + (r + shift) % ranks, b * ranks + r))
    return lax.ppermute(value, ("sub", "rng"), pairs)


def on_device(image, stencil, interp_weights, range_taps):
    beams, columns = image.shape[1:]
    ranks = lax.axis_size("rng")
    total = CHUNKS
    width = columns // total
    table = jnp.transpose(stencil, (0, 1, 2, 4, 3))
    taps = jnp.transpose(range_taps, (2, 1, 0))
    rows = call(functools.partial(edge_kernel, FORWARD[0]), shape((8, beams), f32), (image,))
    back = ranks - 1
    edge_own = swap(rows, None, back)
    edge_other = swap(rows, 0, back)
    partner = swap(image, 0)
    matrix = build((0,), True, table, interp_weights)
    parts = build((1, 2, 3), False, table, interp_weights)
    parts = [parts[k] for k in range(SECTIONS - 1)]
    outer = call(start_kernel, shape((2 * beams, LANES), f32), (matrix, taps, edge_own, edge_other))
    carry = None
    own, other = image, partner
    for s in range(SECTIONS):
        sums = None
        merged, received = [None] * total, [None] * total
        target = None
        for call_num, chunks in enumerate(CALLS[s]):
            outs, left = section(s, chunks, total, width, matrix, taps, carry, outer, sums, own, other, target)
            if call_num + 1 < len(CALLS[s]):
                carry, sums = left
            else:
                (stats,) = left
            if s + 1 == SECTIONS:
                target = outs[0]
                continue
            for chunk, array in zip(chunks, outs):
                merged[chunk] = array
        if s + 1 < SECTIONS:
            for chunk in sum(CALLS[s], ()):
                received[chunk] = swap(merged[chunk], s + 1)
        others, partners = [], []
        for d in range(1, ranks):
            others.append(swap(stats, None, d))
        if s + 1 == SECTIONS:
            factors = call(functools.partial(factor_kernel, ranks), shape((2, beams), f32), [stats] + others)
            return target, factors
        for d in range(ranks):
            partners.append(swap(stats, s + 1, d))
        matrix, outer, *inner = call(
            functools.partial(prep_kernel, s + 1, ranks),
            [shape((2, 2 * beams, 2 * beams), bf16)]
            + [shape((2 * beams, LANES), f32)] * (2 if FORWARD[s + 1] else 1),
            [parts[s], taps, stats, *others, *partners],
        )
        carry = inner[0] if FORWARD[s + 1] else outer
        own, other = merged, received


def solution(mesh):
    placed = (P(None, "sub", "rng"), P(), P(), P())
    return jax.shard_map(
        on_device,
        mesh=mesh,
        in_specs=placed,
        out_specs=(P(None, "sub", "rng"), P(None, "sub")),
        check_vma=False,
    )
```

```python
import functools

import jax
import jax.numpy as jnp
from jax import lax
from jax.experimental import pallas as pl
from jax.experimental.pallas import tpu as pltpu
from jax.sharding import PartitionSpec as P

SECTIONS = 4
TAPS = 4
LANES = 128
epsilon = 1e-06

FORWARD = (True, True, False, False)
SKEW_IN = (0, 1, 2, 1)
CHUNKS = 4
CALLS = (((1,), (2,), (3,), (0,)), ((1, 2, 3), (0,)), ((2,), (1,), (0,), (3,)), ((2,), (1,), (0,), (3,)))
GROUPS = (((1,), (2,), (3,), (0,)), ((2,), (1,), (0,), (3,)), ((2,), (1,), (0,), (3,)))


f32 = jnp.float32
bf16 = jnp.bfloat16
NT = (((1,), (1,)), ((), ()))
VMEM = pl.BlockSpec(memory_space=pltpu.VMEM)


def params(mib=16):
    return pltpu.CompilerParams(vmem_limit_bytes=mib << 20)


def call(kernel, out_shape, args, out_specs=None, in_specs=None, scratch=(), aliases=None, flops=0):
    outs = jax.tree.leaves(out_shape)
    nbytes = sum(a.size * a.dtype.itemsize for a in list(args) + outs)
    return pl.pallas_call(
        kernel,
        out_shape=out_shape,
        in_specs=in_specs or [VMEM] * len(args),
        out_specs=out_specs or jax.tree.map(lambda _: VMEM, out_shape),
        scratch_shapes=list(scratch),
        input_output_aliases=aliases or {},
        compiler_params=params(),
        cost_estimate=pl.CostEstimate(flops=flops, bytes_accessed=nbytes, transcendentals=0),
    )(*args)


def shape(dims, dtype):
    return jax.ShapeDtypeStruct(dims, dtype)


def pair_matrix(out_ref, child, real, imag):
    beams = real.shape[0]
    out_ref[child, :beams, :beams] = real.astype(bf16)
    out_ref[child, :beams, beams:] = (-imag).astype(bf16)
    out_ref[child, beams:, :beams] = imag.astype(bf16)
    out_ref[child, beams:, beams:] = real.astype(bf16)


def angles_kernel(out_ref):
    sub = lax.axis_index("sub")
    beams = out_ref.shape[-1]
    row = lax.broadcasted_iota(jnp.int32, (8, beams), 0)
    beam = lax.broadcasted_iota(jnp.int32, (8, beams), 1).astype(f32)
    angle = jnp.zeros((8, beams), f32)
    sign = jnp.zeros((8, beams), f32)
    for s in range(SECTIONS):
        half = ((sub >> s) & 1).astype(f32)
        here = row % SECTIONS == s
        angle = jnp.where(here, (half * beams + beam + 0.5) * (0.37 + 0.11 * s), angle)
        sign = jnp.where(here, 2.0 * half - 1.0, sign)
    out_ref[...] = jnp.where(row < SECTIONS, jnp.cos(angle), jnp.sin(angle) * sign)


def columns_of(angles_ref, stencil_ref, weights_ref, rows_ref):
    sub = lax.axis_index("sub")
    beams = stencil_ref.shape[-1]
    rows_ref[...] = jnp.zeros_like(rows_ref)
    for s in range(SECTIONS):
        half = (sub >> s) & 1
        cosine = angles_ref[s : s + 1, :]
        sine = angles_ref[SECTIONS + s : SECTIONS + s + 1, :]
        for t in range(TAPS):
            weight = weights_ref[s : s + 1, t : t + 1]
            rows_ref[16 * s + t : 16 * s + t + 1, :] = cosine * weight
            rows_ref[16 * s + 4 + t : 16 * s + 5 + t, :] = sine * weight
        rows_ref[16 * s + 8 : 16 * s + 9, :] = stencil_ref[s, half, half, 0:1, :].astype(f32)
        rows_ref[16 * s + 9 : 16 * s + 10, :] = stencil_ref[s, half, 1 - half, 0:1, :].astype(f32)
    row = lax.broadcasted_iota(jnp.int32, (beams, beams), 0)
    column = lax.broadcasted_iota(jnp.int32, (beams, beams), 1)
    identity = jnp.where(row == column, 1.0, 0.0).astype(bf16)
    return lax.dot_general(identity, rows_ref[...].astype(bf16), NT, preferred_element_type=f32)


def interpolation(columns, s, child):
    beams = columns.shape[0]
    table = columns[:, 16 * s : 16 * s + 16]
    place = lax.broadcasted_iota(jnp.int32, (beams, beams), 1).astype(f32)
    step = place - table[:, 8 + child : 9 + child]
    real = jnp.zeros((beams, beams), f32)
    imag = jnp.zeros((beams, beams), f32)
    for t in range(TAPS):
        hit = step == float(t)
        real = jnp.where(hit, table[:, t : t + 1], real)
        imag = jnp.where(hit, table[:, 4 + t : 5 + t], imag)
    return real, imag if child == 0 else -imag


def build_kernel(angles_ref, stencil_ref, weights_ref, matrix_ref, columns_ref, rows_ref):
    columns = columns_of(angles_ref, stencil_ref, weights_ref, rows_ref)
    columns_ref[...] = columns
    for child in range(2):
        pair_matrix(matrix_ref, child, *interpolation(columns, 0, child))


def parts_kernel(s, columns_ref, out_ref):
    columns = columns_ref[...]
    for child in range(2):
        real, imag = interpolation(columns, s, child)
        out_ref[child, 0] = real.astype(bf16)
        out_ref[child, 1] = imag.astype(bf16)


def edge_rows(forward, tile):
    both = jnp.concatenate([tile[0], tile[1]], axis=1)
    row = lax.broadcasted_iota(jnp.int32, (8, 2 * LANES), 0)
    lane = lax.broadcasted_iota(jnp.int32, (8, 2 * LANES), 1)
    first = LANES - 2 if forward else 0
    wanted = (row - 4) // 2 * LANES + first + (row - 4) % 2
    pick = jnp.where((row >= 4) & (lane == wanted), 1.0, 0.0).astype(bf16)
    return lax.dot_general(pick, both, NT, preferred_element_type=f32)


def edge_kernel(forward, image_ref, partner_ref, out_ref):
    columns = image_ref.shape[-1]
    begin = columns - LANES if forward else 0
    out_ref[0:8, :] = edge_rows(forward, image_ref[:, :, begin : begin + LANES])
    out_ref[8:16, :] = edge_rows(forward, partner_ref[:, :, begin : begin + LANES])


def tap_values(s, taps_ref):
    half = (lax.axis_index("sub") >> s) & 1
    own, other = [], []
    for k in range(3):
        zero = taps_ref[k, 0:1, s : s + 1]
        one = taps_ref[k, 1:2, s : s + 1]
        own.append(jnp.where(half == 1, one, zero))
        other.append(jnp.where(half == 1, zero, one))
    return own, other


def column_terms(s, matrix_ref, taps_ref, edges):
    beams = matrix_ref.shape[1] // 2
    own, other = tap_values(s, taps_ref)
    products = []
    for child in range(2):
        rows = []
        for edge in edges:
            for k in range(2):
                rows.append(
                    jnp.concatenate(
                        [edge[child][4 + k : 5 + k], edge[child][6 + k : 7 + k]], axis=1
                    )
                )
        rows.append(jnp.zeros((LANES - len(rows), 2 * beams), f32))
        rows = jnp.concatenate(rows, axis=0).astype(bf16)
        products.append(
            lax.dot_general(matrix_ref[child], rows, NT, preferred_element_type=f32)
        )
    return [own[k] * products[0] + other[k] * products[1] for k in range(3)]


def carry_of(s, terms, pair, outer=True):
    forward = FORWARD[s]
    lower, middle, upper = terms
    lane = lax.broadcasted_iota(jnp.int32, lower.shape, 1)
    rng = lax.axis_index("rng")
    last = lax.axis_size("rng") - 1
    first = 2 * pair

    def moved(array, source, place):
        shift = (place - source) % LANES
        return pltpu.roll(array, shift, 1) if shift else array

    if forward:
        inner = jnp.where((rng == 0) & (s == 0), 0.0, 1.0) if outer else 1.0
        near = moved(middle, first + 1, 0) + moved(lower, first, 0)
        far = moved(lower, first + 1, 1) * inner
        return jnp.where(lane == 0, near, jnp.where(lane == 1, far, 0.0))
    inner = jnp.where((rng == last) & (s == 3), 0.0, 1.0) if outer else 1.0
    near = moved(middle, first, LANES - 1) + moved(upper, first + 1, LANES - 1) * inner
    far = moved(upper, first, LANES - 2)
    return jnp.where(lane == LANES - 1, near, jnp.where(lane == LANES - 2, far, 0.0))


def factor_rows(refs):
    total = refs[0][0:4]
    for ref in refs[1:]:
        total = total + ref[0:4]
    scale = 1.0 / jnp.sqrt(total[2:3] + epsilon)
    return total[0:1] * scale, -total[1:2] * scale


def factor_kernel(*refs):
    out_ref = refs[-1]
    out_ref[0:1, :], out_ref[1:2, :] = factor_rows(refs[:-1])


def prep_kernel(s, ranks, parts_ref, taps_ref, *refs):
    groups = refs[:ranks], refs[ranks : 2 * ranks]
    matrix_ref, outer_ref, inner_ref = refs[2 * ranks :]
    for child, group in enumerate(groups):
        factor_re, factor_im = factor_rows(group)
        real = parts_ref[child, 0].astype(f32)
        imag = parts_ref[child, 1].astype(f32)
        pair_matrix(
            matrix_ref,
            child,
            real * factor_re - imag * factor_im,
            real * factor_im + imag * factor_re,
        )
    beside = ranks - 1 if FORWARD[s] else 1 % ranks
    edges = [[group[0][8:16] for group in groups], [group[beside][0:8] for group in groups]]
    terms = column_terms(s, matrix_ref, taps_ref, edges)
    inner_ref[...] = carry_of(s, terms, 0, False)
    outer_ref[...] = carry_of(s, terms, 1)


def sum_rows(sums):
    lane = lax.broadcasted_iota(jnp.int32, sums[0].shape, 1)
    table = jnp.zeros(sums[0].shape, f32)
    for k, part in enumerate(sums):
        table = jnp.where(lane == k, jnp.sum(part, axis=1, keepdims=True), table)
    return jnp.transpose(table)[:8]


def section_kernel(s, chunks, groups, places, width, total, first, last, aliased, refs):
    n = len(chunks)
    matrix_ref, taps_ref = refs[:2]
    refs = list(refs[2:])
    carry_ref = None if first and s == 0 else refs.pop(0)
    outmost = 0 if FORWARD[s] else total - 1
    outer_ref = refs.pop(0) if outmost in chunks else None
    sums_ref = None if first else refs.pop(0)

    def view(place):
        number, index = place
        ref = refs[number]
        if isinstance(index, slice):
            return ref.at[:, :, index]
        return ref if index is None else ref.at[index]

    inputs, own_places, other_places, extra_places = places
    own_refs = [view(place) for place in own_places]
    other_refs = [view(place) for place in other_places]
    edges = {chunk: view(place)[...] for chunk, place in extra_places.items()}
    whole_refs = refs[:2]
    rest = refs[inputs + aliased :]
    writes = s + 1 == SECTIONS and not last
    if writes:
        sem, buffer_ref, target_ref = rest.pop(), rest.pop(), rest.pop(0)
        out_refs = [buffer_ref.at[i] for i in range(n)]
    else:
        out_refs = []
        for group in groups:
            ref = rest.pop(0)
            out_refs += [ref] if len(group) == 1 else [ref.at[i] for i in range(len(group))]
        listed = [chunk for group in groups for chunk in group]
        out_refs = [out_refs[listed.index(chunk)] for chunk in chunks]
    if last:
        (stats_out,) = rest
    else:
        carry_out, sums_out = rest
    copies = []
    forward, skew = FORWARD[s], SKEW_IN[s]
    own, other = tap_values(s, taps_ref)
    beams = matrix_ref.shape[1] // 2
    first_rank = lax.axis_index("rng") == 0
    lane = lax.broadcasted_iota(jnp.int32, (1, width), 1)
    if carry_ref is None:
        ends = [edge_rows(True, ref.at[:, :, width - LANES : width]) for ref in whole_refs]
        carry = carry_of(s, column_terms(s, matrix_ref, taps_ref, [ends]), 0, False)
    else:
        carry = carry_ref[...]
    sums = [sums_ref[k] for k in range(3)] if sums_ref is not None else None
    for i, chunk in enumerate(chunks):
        if chunk == outmost and s == 0:
            ends = (outer_ref[0:8], outer_ref[8:16])
            carry = carry_of(s, column_terms(s, matrix_ref, taps_ref, [ends]), 0)
        elif chunk == outmost:
            carry = outer_ref[...]
        own_terms = jnp.dot(
            matrix_ref[0], own_refs[i][...].reshape(2 * beams, width), preferred_element_type=f32
        )
        other_terms = jnp.dot(
            matrix_ref[1], other_refs[i][...].reshape(2 * beams, width), preferred_element_type=f32
        )
        lower, middle, upper = [own[k] * own_terms + other[k] * other_terms for k in range(3)]
        edge = chunk == 0

        def without(array, place):
            if not edge:
                return array
            return jnp.where(first_rank & (lane == place), 0.0, array)

        if forward:
            upper = without(upper, skew)
            rolled1 = pltpu.roll(middle, 1, 1)
            rolled2 = pltpu.roll(lower, 2, 1)
            kept2 = rolled2 if skew == 0 else without(rolled2, skew + 1)
            value = upper + jnp.where(lane >= 1, rolled1, 0.0) + jnp.where(lane >= 2, kept2, 0.0)
            piece = slice(0, LANES)
            lane1 = lane[:, piece]
            following = jnp.where(lane1 < 1, rolled1[:, piece], 0.0) + jnp.where(
                lane1 < 2, rolled2[:, piece], 0.0
            )
        else:
            lower = without(lower, skew - 1)
            rolled1 = pltpu.roll(middle, width - 1, 1)
            rolled2 = pltpu.roll(upper, width - 2, 1)
            kept2 = without(rolled2, skew - 2) if skew >= 2 else rolled2
            value = (
                lower
                + jnp.where(lane < width - 1, rolled1, 0.0)
                + jnp.where(lane < width - 2, kept2, 0.0)
            )
            piece = slice(width - LANES, width)
            lane1 = lane[:, piece]
            following = jnp.where(lane1 >= width - 1, rolled1[:, piece], 0.0) + jnp.where(
                lane1 >= width - 2, rolled2[:, piece], 0.0
            )
        if width == LANES:
            value = value + carry
        elif forward:
            value = jnp.concatenate([value[:, :LANES] + carry, value[:, LANES:]], axis=1)
        else:
            value = jnp.concatenate([value[:, : width - LANES], value[:, width - LANES :] + carry], axis=1)
        carry = following
        merged = value.astype(bf16)
        out_refs[i][0] = merged[:beams]
        out_refs[i][1] = merged[beams:]
        if writes:
            place = target_ref.at[:, :, chunk * width : (chunk + 1) * width]
            copies.append(pltpu.make_async_copy(buffer_ref.at[i], place, sem.at[i]))
            copies[-1].start()
        v0 = merged[:beams].astype(f32)
        v1 = merged[beams:].astype(f32)
        f0 = pltpu.roll(v0, beams - 1, 0)
        f1 = pltpu.roll(v1, beams - 1, 0)
        lag_real = v0 * f0 + v1 * f1
        lag_imag = v0 * f1 - v1 * f0
        power = (v0 * v0 + v1 * v1) * (f0 * f0 + f1 * f1)
        folded = []
        for product in (lag_real, lag_imag, power):
            part = product[:, :LANES]
            for k in range(1, width // LANES):
                part = part + product[:, k * LANES : (k + 1) * LANES]
            folded.append(part)
        sums = folded if sums is None else [x + y for x, y in zip(sums, folded)]
        edges[chunk] = merged.reshape(2, beams, width)
    if last:
        stats = sum_rows(sums)
        if s + 1 < SECTIONS:
            onward = FORWARD[s + 1]
            begin = width - LANES if onward else 0
            ends = [edge_rows(onward, edges[c][:, :, begin : begin + LANES]) for c in (0, total - 1)]
            inner, outer = ends if onward else ends[::-1]
            stats = jnp.concatenate([stats + outer, inner], axis=0)
        stats_out[...] = stats
    else:
        carry_out[...] = carry
        for k in range(3):
            sums_out[k] = sums[k]
    for copy in copies:
        copy.wait()


def section(s, chunks, total, width, matrix, taps, carry, outer, sums, own, other, merged, target):
    n = len(chunks)
    beams = matrix.shape[1] // 2
    first = sums is None
    last = chunks == CALLS[s][-1]
    args = [matrix, taps]
    if carry is not None:
        args.append(carry)
    if (0 if FORWARD[s] else total - 1) in chunks:
        args.append(outer)
    if not first:
        args.append(sums)
    specs = [VMEM] * len(args)
    final = s + 1 == SECTIONS
    arrays = []

    def place_of(array, index):
        for number, known in enumerate(arrays):
            if known is array:
                return number, index
        arrays.append(array)
        return len(arrays) - 1, index

    own_places = [place_of(*own[chunk]) for chunk in chunks]
    other_places = [place_of(*other[chunk]) for chunk in chunks]
    extra_places = {}
    if last and not final:
        extra_places = {
            chunk: place_of(*merged[chunk]) for chunk in (0, total - 1) if chunk not in chunks
        }
    places = (len(arrays), own_places, other_places, extra_places)
    args += arrays
    specs += [VMEM] * len(arrays)
    groups = [chunks] if final else [group for group in GROUPS[s] if group[0] in chunks]
    aliases = {}
    scratch = []
    if final and not last:
        outs = [shape((2, beams, total * width), bf16)]
        blocks = [pl.BlockSpec(memory_space=pl.ANY)]
        scratch = [pltpu.VMEM((n, 2, beams, width), bf16), pltpu.SemaphoreType.DMA((n,))]
        if target is not None:
            aliases = {len(args): 0}
            args.append(target)
            specs.append(pl.BlockSpec(memory_space=pl.ANY))
    else:
        outs = [
            shape((2, beams, width) if len(group) == 1 else (len(group), 2, beams, width), bf16)
            for group in groups
        ]
        blocks = [VMEM] * len(outs)
    images = len(outs)
    if last:
        outs = outs + [shape((8 if final else 16, beams), f32)]
    else:
        outs = outs + [shape((2 * beams, LANES), f32), shape((3, beams, LANES), f32)]
    blocks = blocks + [VMEM] * (len(outs) - images)
    result = call(
        lambda *refs: section_kernel(s, chunks, groups, places, width, total, first, last, len(aliases), refs),
        outs,
        args,
        out_specs=blocks,
        in_specs=specs,
        scratch=scratch,
        aliases=aliases,
        flops=n * 2 * 2 * (2 * beams) ** 2 * width,
    )
    images, left = result[:images], result[images:]
    for group, array in zip(groups, images):
        for index, chunk in enumerate(group):
            merged[chunk] = (array, None if len(group) == 1 else index)
    return images, left


def write_kernel(chunk, value_ref, target_in, target_ref, sem):
    width = value_ref.shape[-1]
    copy = pltpu.make_async_copy(value_ref, target_ref.at[:, :, chunk * width : (chunk + 1) * width], sem)
    copy.start()
    copy.wait()


def swap(value, s, shift=0):
    size, ranks = lax.axis_size("sub"), lax.axis_size("rng")
    mask = 0 if s is None else 2**s
    pairs = []
    for b in range(size):
        for r in range(ranks):
            pairs.append(((b ^ mask) * ranks + (r + shift) % ranks, b * ranks + r))
    return lax.ppermute(value, ("sub", "rng"), pairs)


def on_device(image, stencil, interp_weights, range_taps):
    beams, columns = image.shape[1:]
    ranks = lax.axis_size("rng")
    total = CHUNKS
    width = columns // total
    table = jnp.transpose(stencil, (0, 1, 2, 4, 3))
    taps = jnp.transpose(range_taps, (2, 1, 0))
    partner = swap(image, 0)
    angles = call(angles_kernel, shape((8, beams), f32), (), flops=10**10)
    matrix, table = call(
        build_kernel,
        [shape((2, 2 * beams, 2 * beams), bf16), shape((beams, 16 * SECTIONS), f32)],
        (angles, table, interp_weights),
        scratch=[pltpu.VMEM((16 * SECTIONS, beams), f32)],
    )
    parts = [None]
    for s in range(1, SECTIONS):
        parts.append(call(functools.partial(parts_kernel, s), shape((2, 2, beams, beams), bf16), (table,)))
    rows = call(functools.partial(edge_kernel, FORWARD[0]), shape((16, beams), f32), (image, partner))
    outer = swap(rows, None, ranks - 1)
    carry = None
    cuts = [slice(chunk * width, (chunk + 1) * width) for chunk in range(total)]
    own, other = [(image, cut) for cut in cuts], [(partner, cut) for cut in cuts]
    for s in range(SECTIONS):
        sums = target = None
        merged, received = [None] * total, [None] * total
        for call_num, chunks in enumerate(CALLS[s]):
            outs, left = section(s, chunks, total, width, matrix, taps, carry, outer, sums, own, other, merged, target)
            if call_num + 1 < len(CALLS[s]):
                carry, sums = left
            else:
                (stats,) = left
            if len(outs) == 1 and s + 1 == SECTIONS:
                target = outs[0] if call_num + 1 < len(CALLS[s]) else target
        others = []
        for d in range(1, ranks):
            others.append(swap(stats, None, d))
        if s + 1 == SECTIONS:
            target = call(
                functools.partial(write_kernel, CALLS[s][-1][0]),
                shape((2, beams, columns), bf16),
                [outs[0], target],
                in_specs=[VMEM, pl.BlockSpec(memory_space=pl.ANY)],
                out_specs=pl.BlockSpec(memory_space=pl.ANY),
                scratch=[pltpu.SemaphoreType.DMA],
                aliases={1: 0},
            )
            factors = call(factor_kernel, shape((2, beams), f32), [stats] + others)
            return target, factors
        given = []
        for d in range(ranks):
            given.append(swap(stats, s + 1, d))
        for group in GROUPS[s]:
            array = swap(merged[group[0]][0], s + 1)
            for chunk in group:
                received[chunk] = (array, merged[chunk][1])
        matrix, outer, carry = call(
            functools.partial(prep_kernel, s + 1, ranks),
            [shape((2, 2 * beams, 2 * beams), bf16)] + [shape((2 * beams, LANES), f32)] * 2,
            [parts[s + 1], taps, stats, *others, *given],
        )
        own, other = merged, received


def solution(mesh):
    placed = (P(None, "sub", "rng"), P(), P(), P())
    return jax.shard_map(
        on_device,
        mesh=mesh,
        in_specs=placed,
        out_specs=(P(None, "sub", "rng"), P(None, "sub")),
        check_vma=False,
    )
```

```python
import functools

import jax
import jax.numpy as jnp
from jax import lax
from jax.experimental import pallas as pl
from jax.experimental.pallas import tpu as pltpu
from jax.sharding import PartitionSpec as P

SECTIONS = 4
TAPS = 4
LANES = 128
epsilon = 1e-06

FORWARD = (True, True, False, False)
SKEW_IN = (0, 1, 2, 1)
CHUNKS = 4
CALLS = (((1,), (2,), (3,), (0,)), ((1, 2, 3), (0,)), ((2,), (1,), (0,), (3,)), ((2,), (1,), (0,), (3,)))
GROUPS = (((1,), (2,), (3,), (0,)), ((2,), (1,), (0,), (3,)), ((2,), (1,), (0,), (3,)))


f32 = jnp.float32
bf16 = jnp.bfloat16
NT = (((1,), (1,)), ((), ()))
VMEM = pl.BlockSpec(memory_space=pltpu.VMEM)


def params(mib=16):
    return pltpu.CompilerParams(vmem_limit_bytes=mib << 20)


def call(kernel, out_shape, args, out_specs=None, in_specs=None, scratch=(), aliases=None, flops=0):
    outs = jax.tree.leaves(out_shape)
    nbytes = sum(a.size * a.dtype.itemsize for a in list(args) + outs)
    return pl.pallas_call(
        kernel,
        out_shape=out_shape,
        in_specs=in_specs or [VMEM] * len(args),
        out_specs=out_specs or jax.tree.map(lambda _: VMEM, out_shape),
        scratch_shapes=list(scratch),
        input_output_aliases=aliases or {},
        compiler_params=params(),
        cost_estimate=pl.CostEstimate(flops=flops, bytes_accessed=nbytes, transcendentals=0),
    )(*args)


def shape(dims, dtype):
    return jax.ShapeDtypeStruct(dims, dtype)


def pair_matrix(out_ref, child, real, imag):
    beams = real.shape[0]
    out_ref[child, :beams, :beams] = real.astype(bf16)
    out_ref[child, :beams, beams:] = (-imag).astype(bf16)
    out_ref[child, beams:, :beams] = imag.astype(bf16)
    out_ref[child, beams:, beams:] = real.astype(bf16)


def angles_kernel(out_ref):
    sub = lax.axis_index("sub")
    beams = out_ref.shape[-1]
    row = lax.broadcasted_iota(jnp.int32, (8, beams), 0)
    beam = lax.broadcasted_iota(jnp.int32, (8, beams), 1).astype(f32)
    angle = jnp.zeros((8, beams), f32)
    sign = jnp.zeros((8, beams), f32)
    for s in range(SECTIONS):
        half = ((sub >> s) & 1).astype(f32)
        here = row % SECTIONS == s
        angle = jnp.where(here, (half * beams + beam + 0.5) * (0.37 + 0.11 * s), angle)
        sign = jnp.where(here, 2.0 * half - 1.0, sign)
    out_ref[...] = jnp.where(row < SECTIONS, jnp.cos(angle), jnp.sin(angle) * sign)


def columns_of(angles_ref, stencil_ref, weights_ref, rows_ref):
    sub = lax.axis_index("sub")
    beams = stencil_ref.shape[-1]
    rows_ref[...] = jnp.zeros_like(rows_ref)
    for s in range(SECTIONS):
        half = (sub >> s) & 1
        cosine = angles_ref[s : s + 1, :]
        sine = angles_ref[SECTIONS + s : SECTIONS + s + 1, :]
        for t in range(TAPS):
            weight = weights_ref[s : s + 1, t : t + 1]
            rows_ref[16 * s + t : 16 * s + t + 1, :] = cosine * weight
            rows_ref[16 * s + 4 + t : 16 * s + 5 + t, :] = sine * weight
        rows_ref[16 * s + 8 : 16 * s + 9, :] = stencil_ref[s, half, half, 0:1, :].astype(f32)
        rows_ref[16 * s + 9 : 16 * s + 10, :] = stencil_ref[s, half, 1 - half, 0:1, :].astype(f32)
    row = lax.broadcasted_iota(jnp.int32, (beams, beams), 0)
    column = lax.broadcasted_iota(jnp.int32, (beams, beams), 1)
    identity = jnp.where(row == column, 1.0, 0.0).astype(bf16)
    return lax.dot_general(identity, rows_ref[...].astype(bf16), NT, preferred_element_type=f32)


def interpolation(columns, s, child):
    beams = columns.shape[0]
    table = columns[:, 16 * s : 16 * s + 16]
    place = lax.broadcasted_iota(jnp.int32, (beams, beams), 1).astype(f32)
    step = place - table[:, 8 + child : 9 + child]
    real = jnp.zeros((beams, beams), f32)
    imag = jnp.zeros((beams, beams), f32)
    for t in range(TAPS):
        hit = step == float(t)
        real = jnp.where(hit, table[:, t : t + 1], real)
        imag = jnp.where(hit, table[:, 4 + t : 5 + t], imag)
    return real, imag if child == 0 else -imag


def build_kernel(angles_ref, stencil_ref, weights_ref, matrix_ref, columns_ref, rows_ref):
    columns = columns_of(angles_ref, stencil_ref, weights_ref, rows_ref)
    columns_ref[...] = columns
    for child in range(2):
        pair_matrix(matrix_ref, child, *interpolation(columns, 0, child))


def parts_kernel(s, columns_ref, out_ref):
    columns = columns_ref[...]
    for child in range(2):
        real, imag = interpolation(columns, s, child)
        out_ref[child, 0] = real.astype(bf16)
        out_ref[child, 1] = imag.astype(bf16)


def edge_rows(forward, tile):
    both = jnp.concatenate([tile[0], tile[1]], axis=1)
    row = lax.broadcasted_iota(jnp.int32, (8, 2 * LANES), 0)
    lane = lax.broadcasted_iota(jnp.int32, (8, 2 * LANES), 1)
    first = LANES - 2 if forward else 0
    wanted = (row - 4) // 2 * LANES + first + (row - 4) % 2
    pick = jnp.where((row >= 4) & (lane == wanted), 1.0, 0.0).astype(bf16)
    return lax.dot_general(pick, both, NT, preferred_element_type=f32)


def edge_kernel(forward, image_ref, partner_ref, out_ref):
    columns = image_ref.shape[-1]
    begin = columns - LANES if forward else 0
    out_ref[0:8, :] = edge_rows(forward, image_ref[:, :, begin : begin + LANES])
    out_ref[8:16, :] = edge_rows(forward, partner_ref[:, :, begin : begin + LANES])


def tap_values(s, taps_ref):
    half = (lax.axis_index("sub") >> s) & 1
    own, other = [], []
    for k in range(3):
        zero = taps_ref[k, 0:1, s : s + 1]
        one = taps_ref[k, 1:2, s : s + 1]
        own.append(jnp.where(half == 1, one, zero))
        other.append(jnp.where(half == 1, zero, one))
    return own, other


def column_terms(s, matrix_ref, taps_ref, edges):
    beams = matrix_ref.shape[1] // 2
    own, other = tap_values(s, taps_ref)
    products = []
    for child in range(2):
        rows = []
        for edge in edges:
            for k in range(2):
                rows.append(
                    jnp.concatenate(
                        [edge[child][4 + k : 5 + k], edge[child][6 + k : 7 + k]], axis=1
                    )
                )
        rows.append(jnp.zeros((LANES - len(rows), 2 * beams), f32))
        rows = jnp.concatenate(rows, axis=0).astype(bf16)
        products.append(
            lax.dot_general(matrix_ref[child], rows, NT, preferred_element_type=f32)
        )
    return [own[k] * products[0] + other[k] * products[1] for k in range(3)]


def carry_of(s, terms, pair, outer=True):
    forward = FORWARD[s]
    lower, middle, upper = terms
    lane = lax.broadcasted_iota(jnp.int32, lower.shape, 1)
    rng = lax.axis_index("rng")
    last = lax.axis_size("rng") - 1
    first = 2 * pair

    def moved(array, source, place):
        shift = (place - source) % LANES
        return pltpu.roll(array, shift, 1) if shift else array

    if forward:
        inner = jnp.where((rng == 0) & (s == 0), 0.0, 1.0) if outer else 1.0
        near = moved(middle, first + 1, 0) + moved(lower, first, 0)
        far = moved(lower, first + 1, 1) * inner
        return jnp.where(lane == 0, near, jnp.where(lane == 1, far, 0.0))
    inner = jnp.where((rng == last) & (s == 3), 0.0, 1.0) if outer else 1.0
    near = moved(middle, first, LANES - 1) + moved(upper, first + 1, LANES - 1) * inner
    far = moved(upper, first, LANES - 2)
    return jnp.where(lane == LANES - 1, near, jnp.where(lane == LANES - 2, far, 0.0))


def factor_rows(refs):
    total = refs[0][0:4]
    for ref in refs[1:]:
        total = total + ref[0:4]
    scale = 1.0 / jnp.sqrt(total[2:3] + epsilon)
    return total[0:1] * scale, -total[1:2] * scale


def factor_kernel(*refs):
    out_ref = refs[-1]
    out_ref[0:1, :], out_ref[1:2, :] = factor_rows(refs[:-1])


def prep_kernel(s, ranks, parts_ref, taps_ref, *refs):
    groups = refs[:ranks], refs[ranks : 2 * ranks]
    matrix_ref, outer_ref, inner_ref = refs[2 * ranks :]
    for child, group in enumerate(groups):
        factor_re, factor_im = factor_rows(group)
        real = parts_ref[child, 0].astype(f32)
        imag = parts_ref[child, 1].astype(f32)
        pair_matrix(
            matrix_ref,
            child,
            real * factor_re - imag * factor_im,
            real * factor_im + imag * factor_re,
        )
    beside = ranks - 1 if FORWARD[s] else 1 % ranks
    edges = [[group[0][8:16] for group in groups], [group[beside][0:8] for group in groups]]
    terms = column_terms(s, matrix_ref, taps_ref, edges)
    inner_ref[...] = carry_of(s, terms, 0, False)
    outer_ref[...] = carry_of(s, terms, 1)


def sum_rows(sums):
    lane = lax.broadcasted_iota(jnp.int32, sums[0].shape, 1)
    table = jnp.zeros(sums[0].shape, f32)
    for k, part in enumerate(sums):
        table = jnp.where(lane == k, jnp.sum(part, axis=1, keepdims=True), table)
    return jnp.transpose(table)[:8]


def section_kernel(s, chunks, groups, places, width, total, first, last, aliased, refs):
    n = len(chunks)
    matrix_ref, taps_ref = refs[:2]
    refs = list(refs[2:])
    carry_ref = None if first and s == 0 else refs.pop(0)
    outmost = 0 if FORWARD[s] else total - 1
    outer_ref = refs.pop(0) if outmost in chunks else None
    sums_ref = None if first else refs.pop(0)

    def view(place):
        number, index = place
        ref = refs[number]
        if isinstance(index, slice):
            return ref.at[:, :, index]
        return ref if index is None else ref.at[index]

    inputs, own_places, other_places, extra_places = places
    own_refs = [view(place) for place in own_places]
    other_refs = [view(place) for place in other_places]
    edges = {chunk: view(place)[...] for chunk, place in extra_places.items()}
    whole_refs = refs[:2]
    rest = refs[inputs + aliased :]
    writes = s + 1 == SECTIONS and not last
    if writes:
        sem, buffer_ref, target_ref = rest.pop(), rest.pop(), rest.pop(0)
        out_refs = [buffer_ref.at[i] for i in range(n)]
    else:
        out_refs = []
        for group in groups:
            ref = rest.pop(0)
            out_refs += [ref] if len(group) == 1 else [ref.at[i] for i in range(len(group))]
        listed = [chunk for group in groups for chunk in group]
        out_refs = [out_refs[listed.index(chunk)] for chunk in chunks]
    if last:
        (stats_out,) = rest
    else:
        carry_out, sums_out = rest
    copies = []
    forward, skew = FORWARD[s], SKEW_IN[s]
    own, other = tap_values(s, taps_ref)
    beams = matrix_ref.shape[1] // 2
    first_rank = lax.axis_index("rng") == 0
    lane = lax.broadcasted_iota(jnp.int32, (1, width), 1)
    if carry_ref is None:
        ends = [
            jnp.dot(
                matrix_ref[child],
                whole_refs[child][:, :, width - LANES : width].reshape(2 * beams, LANES),
                preferred_element_type=f32,
            )
            for child in range(2)
        ]
        terms = [own[k] * ends[0] + other[k] * ends[1] for k in range(3)]
        carry = carry_of(s, terms, LANES // 2 - 1, False)
    else:
        carry = carry_ref[...]
    sums = [sums_ref[k] for k in range(3)] if sums_ref is not None else None
    for i, chunk in enumerate(chunks):
        if chunk == outmost and s == 0:
            ends = (outer_ref[0:8], outer_ref[8:16])
            carry = carry_of(s, column_terms(s, matrix_ref, taps_ref, [ends]), 0)
        elif chunk == outmost:
            carry = outer_ref[...]
        own_terms = jnp.dot(
            matrix_ref[0], own_refs[i][...].reshape(2 * beams, width), preferred_element_type=f32
        )
        other_terms = jnp.dot(
            matrix_ref[1], other_refs[i][...].reshape(2 * beams, width), preferred_element_type=f32
        )
        lower, middle, upper = [own[k] * own_terms + other[k] * other_terms for k in range(3)]
        edge = chunk == 0

        def without(array, place):
            if not edge:
                return array
            return jnp.where(first_rank & (lane == place), 0.0, array)

        if forward:
            upper = without(upper, skew)
            rolled1 = pltpu.roll(middle, 1, 1)
            rolled2 = pltpu.roll(lower, 2, 1)
            kept2 = rolled2 if skew == 0 else without(rolled2, skew + 1)
            value = upper + jnp.where(lane >= 1, rolled1, 0.0) + jnp.where(lane >= 2, kept2, 0.0)
            piece = slice(0, LANES)
            lane1 = lane[:, piece]
            following = jnp.where(lane1 < 1, rolled1[:, piece], 0.0) + jnp.where(
                lane1 < 2, rolled2[:, piece], 0.0
            )
        else:
            lower = without(lower, skew - 1)
            rolled1 = pltpu.roll(middle, width - 1, 1)
            rolled2 = pltpu.roll(upper, width - 2, 1)
            kept2 = without(rolled2, skew - 2) if skew >= 2 else rolled2
            value = (
                lower
                + jnp.where(lane < width - 1, rolled1, 0.0)
                + jnp.where(lane < width - 2, kept2, 0.0)
            )
            piece = slice(width - LANES, width)
            lane1 = lane[:, piece]
            following = jnp.where(lane1 >= width - 1, rolled1[:, piece], 0.0) + jnp.where(
                lane1 >= width - 2, rolled2[:, piece], 0.0
            )
        if width == LANES:
            value = value + carry
        elif forward:
            value = jnp.concatenate([value[:, :LANES] + carry, value[:, LANES:]], axis=1)
        else:
            value = jnp.concatenate([value[:, : width - LANES], value[:, width - LANES :] + carry], axis=1)
        carry = following
        merged = value.astype(bf16)
        out_refs[i][0] = merged[:beams]
        out_refs[i][1] = merged[beams:]
        if writes:
            place = target_ref.at[:, :, chunk * width : (chunk + 1) * width]
            copies.append(pltpu.make_async_copy(buffer_ref.at[i], place, sem.at[i]))
            copies[-1].start()
        v0 = merged[:beams].astype(f32)
        v1 = merged[beams:].astype(f32)
        f0 = pltpu.roll(v0, beams - 1, 0)
        f1 = pltpu.roll(v1, beams - 1, 0)
        lag_real = v0 * f0 + v1 * f1
        lag_imag = v0 * f1 - v1 * f0
        power = (v0 * v0 + v1 * v1) * (f0 * f0 + f1 * f1)
        folded = []
        for product in (lag_real, lag_imag, power):
            part = product[:, :LANES]
            for k in range(1, width // LANES):
                part = part + product[:, k * LANES : (k + 1) * LANES]
            folded.append(part)
        sums = folded if sums is None else [x + y for x, y in zip(sums, folded)]
        edges[chunk] = merged.reshape(2, beams, width)
    if last:
        stats = sum_rows(sums)
        if s + 1 < SECTIONS:
            onward = FORWARD[s + 1]
            begin = width - LANES if onward else 0
            ends = [edge_rows(onward, edges[c][:, :, begin : begin + LANES]) for c in (0, total - 1)]
            inner, outer = ends if onward else ends[::-1]
            stats = jnp.concatenate([stats + outer, inner], axis=0)
        stats_out[...] = stats
    else:
        carry_out[...] = carry
        for k in range(3):
            sums_out[k] = sums[k]
    for copy in copies:
        copy.wait()


def section(s, chunks, total, width, matrix, taps, carry, outer, sums, own, other, merged, target):
    n = len(chunks)
    beams = matrix.shape[1] // 2
    first = sums is None
    last = chunks == CALLS[s][-1]
    args = [matrix, taps]
    if carry is not None:
        args.append(carry)
    if (0 if FORWARD[s] else total - 1) in chunks:
        args.append(outer)
    if not first:
        args.append(sums)
    specs = [VMEM] * len(args)
    final = s + 1 == SECTIONS
    arrays = []

    def place_of(array, index):
        for number, known in enumerate(arrays):
            if known is array:
                return number, index
        arrays.append(array)
        return len(arrays) - 1, index

    own_places = [place_of(*own[chunk]) for chunk in chunks]
    other_places = [place_of(*other[chunk]) for chunk in chunks]
    extra_places = {}
    if last and not final:
        extra_places = {
            chunk: place_of(*merged[chunk]) for chunk in (0, total - 1) if chunk not in chunks
        }
    places = (len(arrays), own_places, other_places, extra_places)
    args += arrays
    specs += [VMEM] * len(arrays)
    groups = [chunks] if final else [group for group in GROUPS[s] if group[0] in chunks]
    aliases = {}
    scratch = []
    if final and not last:
        outs = [shape((2, beams, total * width), bf16)]
        blocks = [pl.BlockSpec(memory_space=pl.ANY)]
        scratch = [pltpu.VMEM((n, 2, beams, width), bf16), pltpu.SemaphoreType.DMA((n,))]
        if target is not None:
            aliases = {len(args): 0}
            args.append(target)
            specs.append(pl.BlockSpec(memory_space=pl.ANY))
    else:
        outs = [
            shape((2, beams, width) if len(group) == 1 else (len(group), 2, beams, width), bf16)
            for group in groups
        ]
        blocks = [VMEM] * len(outs)
    images = len(outs)
    if last:
        outs = outs + [shape((8 if final else 16, beams), f32)]
    else:
        outs = outs + [shape((2 * beams, LANES), f32), shape((3, beams, LANES), f32)]
    blocks = blocks + [VMEM] * (len(outs) - images)
    result = call(
        lambda *refs: section_kernel(s, chunks, groups, places, width, total, first, last, len(aliases), refs),
        outs,
        args,
        out_specs=blocks,
        in_specs=specs,
        scratch=scratch,
        aliases=aliases,
        flops=n * 2 * 2 * (2 * beams) ** 2 * width,
    )
    images, left = result[:images], result[images:]
    for group, array in zip(groups, images):
        for index, chunk in enumerate(group):
            merged[chunk] = (array, None if len(group) == 1 else index)
    return images, left


def write_kernel(chunk, value_ref, target_in, target_ref, sem):
    width = value_ref.shape[-1]
    copy = pltpu.make_async_copy(value_ref, target_ref.at[:, :, chunk * width : (chunk + 1) * width], sem)
    copy.start()
    copy.wait()


def swap(value, s, shift=0):
    size, ranks = lax.axis_size("sub"), lax.axis_size("rng")
    mask = 0 if s is None else 2**s
    pairs = []
    for b in range(size):
        for r in range(ranks):
            pairs.append(((b ^ mask) * ranks + (r + shift) % ranks, b * ranks + r))
    return lax.ppermute(value, ("sub", "rng"), pairs)


def on_device(image, stencil, interp_weights, range_taps):
    beams, columns = image.shape[1:]
    ranks = lax.axis_size("rng")
    total = CHUNKS
    width = columns // total
    table = jnp.transpose(stencil, (0, 1, 2, 4, 3))
    taps = jnp.transpose(range_taps, (2, 1, 0))
    partner = swap(image, 0)
    angles = call(angles_kernel, shape((8, beams), f32), (), flops=10**10)
    matrix, table = call(
        build_kernel,
        [shape((2, 2 * beams, 2 * beams), bf16), shape((beams, 16 * SECTIONS), f32)],
        (angles, table, interp_weights),
        scratch=[pltpu.VMEM((16 * SECTIONS, beams), f32)],
        flops=10**10,
    )
    parts = [None]
    for s in range(1, SECTIONS):
        parts.append(call(functools.partial(parts_kernel, s), shape((2, 2, beams, beams), bf16), (table,)))
    rows = call(functools.partial(edge_kernel, FORWARD[0]), shape((16, beams), f32), (image, partner))
    outer = swap(rows, None, ranks - 1)
    carry = None
    cuts = [slice(chunk * width, (chunk + 1) * width) for chunk in range(total)]
    own, other = [(image, cut) for cut in cuts], [(partner, cut) for cut in cuts]
    for s in range(SECTIONS):
        sums = target = None
        merged, received = [None] * total, [None] * total
        for call_num, chunks in enumerate(CALLS[s]):
            outs, left = section(s, chunks, total, width, matrix, taps, carry, outer, sums, own, other, merged, target)
            if call_num + 1 < len(CALLS[s]):
                carry, sums = left
            else:
                (stats,) = left
            if len(outs) == 1 and s + 1 == SECTIONS:
                target = outs[0] if call_num + 1 < len(CALLS[s]) else target
        others = []
        for d in range(1, ranks):
            others.append(swap(stats, None, d))
        if s + 1 == SECTIONS:
            target = call(
                functools.partial(write_kernel, CALLS[s][-1][0]),
                shape((2, beams, columns), bf16),
                [outs[0], target],
                in_specs=[VMEM, pl.BlockSpec(memory_space=pl.ANY)],
                out_specs=pl.BlockSpec(memory_space=pl.ANY),
                scratch=[pltpu.SemaphoreType.DMA],
                aliases={1: 0},
            )
            factors = call(factor_kernel, shape((2, beams), f32), [stats] + others)
            return target, factors
        given = []
        for d in range(ranks):
            given.append(swap(stats, s + 1, d))
        for group in GROUPS[s]:
            array = swap(merged[group[0]][0], s + 1)
            for chunk in group:
                received[chunk] = (array, merged[chunk][1])
        matrix, outer, carry = call(
            functools.partial(prep_kernel, s + 1, ranks),
            [shape((2, 2 * beams, 2 * beams), bf16)] + [shape((2 * beams, LANES), f32)] * 2,
            [parts[s + 1], taps, stats, *others, *given],
        )
        own, other = merged, received


def solution(mesh):
    placed = (P(None, "sub", "rng"), P(), P(), P())
    return jax.shard_map(
        on_device,
        mesh=mesh,
        in_specs=placed,
        out_specs=(P(None, "sub", "rng"), P(None, "sub")),
        check_vma=False,
    )
```
